32 devices in a mesh: dom: 4 (over y, x), col: 8 (over z, core).
Axes of the slice: x: 2, y: 2, z: 4, core: 2. Of those that a mesh axis runs over, the one named last changes fastest.
Arguments:
- ensemble: float32 [128, 5, 96, 1024], P('dom', None, None, 'col'), may hold values from -6 to 6
- depth_class: int32 [96, 1024], P(None, 'col'), may hold values from 0 to 7
- obs_index: int32 [6144], P('col'), may hold values from 0 to 12287
- obs_value: float32 [6144], P('col'), may hold values from -4 to 16
- annealing_exponents: float32 [96, 1024], P(None, 'col'), may hold values from 0.05 to 1
Outputs:
- posterior: float32 [5, 96, 1024], P(None, None, 'col')
The draws below stay inside these ranges and needn't reach their ends.
Inputs may be any that keep to these rules, and one draw needn't show every extreme that they name: `obs_index`: each entry is a cell of its own block of 128 columns, numbered row * 128 + column within the block; entries may repeat.
All inputs are finite; a program needn't handle non-finite values.
Results may differ from the reference program's by a relative error of at most 0.0003.
Values sent between devices are 32-bit elements; how exact they have to be, the bound alone decides.
No kernel may reach another device: no remote copies, remote signals or barrier semaphores. Data moves between devices by JAX's collectives and lax.ppermute only.
A program may use at most 128 MiB of HBM per device.

```python
import math
import jax
import jax.numpy as jnp
from jax import lax

FIELDS = 5
ROWS = 96
COL_DEV = 128
ROW_REACH = 8
RADIUS = 64
OBS_DEV = 768
MEMBERS = 128
COLS = 1024
NOBS = 6144
N_COL = 8


def draw_annealing_exponents(key, part):
    unit = jax.random.uniform(key, (ROWS, COLS), jnp.float32)
    return jnp.exp(math.log(0.05) + unit * math.log(20.0))


def draw_obs_value(key, part):
    blocks = NOBS // OBS_DEV
    key_noise = jax.random.fold_in(key, 11)
    key_bits = jax.random.fold_in(key, 12)
    key_pick = jax.random.fold_in(key, 13)
    bits_drawn = jax.random.randint(key_bits, (blocks,), 0, 2)
    forced = jax.random.randint(key_pick, (), 0, blocks)
    chosen = jnp.maximum(bits_drawn, (jnp.arange(blocks) == forced).astype(jnp.int32))
    offset = 12.0 * chosen.astype(jnp.float32)
    noise = jnp.clip(jax.random.normal(key_noise, (blocks, OBS_DEV), jnp.float32), -4.0, 4.0)
    return (noise + offset[:, None]).reshape(NOBS)


def set_ends(result, key, least, high):
    spot = [jax.random.randint(jax.random.fold_in(key, axis), (), 0, length) for axis, length in enumerate(result.shape)]
    widest = result.shape.index(max(result.shape))
    beside = spot[:widest] + [(spot[widest] + 1) % result.shape[widest]] + spot[widest + 1:]
    return result.at[tuple(spot)].set(least).at[tuple(beside)].set(high)


def shard_levels(key, dims, pieces, low, largest):
    def one(dim, parts):
        steps = jax.random.uniform(jax.random.fold_in(jax.random.fold_in(key, 6), dim), (parts,), jnp.float32, low / len(pieces), largest / len(pieces))
        return jnp.repeat(jnp.exp(steps), dims[dim] // parts).reshape((-1,) + (1,) * (len(dims) - dim - 1))

    level = one(*pieces[0])
    for cut in pieces[1:]:
        level = level * one(*cut)
    return level


def bell_draw(own_key, dims, width, most, pieces=(), kind=jnp.bfloat16):
    values = jax.random.normal(own_key, dims, jnp.float32) * width
    if len(pieces) > 0:
        values = shard_levels(own_key, dims, pieces, -0.22, 0.18) * values
    return jnp.clip(values, min=-most, max=most).astype(kind)


def setup_inputs(seed: int = 0) -> dict:
    arg_keys = jax.random.split(jax.random.key(seed), 6)
    ensemble = bell_draw(arg_keys[0], (MEMBERS, FIELDS, ROWS, COLS), 1.0, 6.0, ((0, 4), (3, 8)), jnp.float32)
    depth_class = set_ends(jax.random.randint(arg_keys[1], (ROWS, COLS), 0, 8), jax.random.fold_in(arg_keys[1], 1), 0, 7).astype(jnp.int32)
    obs_index = set_ends(jax.random.randint(arg_keys[2], (NOBS,), 0, ROWS * COL_DEV), jax.random.fold_in(arg_keys[2], 1), 0, (ROWS * COL_DEV) - 1).astype(jnp.int32)
    obs_value = draw_obs_value(jax.random.fold_in(arg_keys[5], 71), 0)
    annealing_exponents = draw_annealing_exponents(jax.random.fold_in(arg_keys[5], 71), 0)
    return {"ensemble": ensemble, "depth_class": depth_class, "obs_index": obs_index, "obs_value": obs_value, "annealing_exponents": annealing_exponents}


TIME_STEP = 0.25
CORIOLIS = 0.2


def diff_cols(field):
    return 0.5 * (field[..., 2:] - field[..., :-2])


def diff_rows(field):
    padded = jnp.pad(field, [(0, 0)] * (field.ndim - 2) + [(1, 1), (0, 0)])
    return 0.5 * (padded[..., 2:, :] - padded[..., :-2, :])


def integrate_model_ahead(solution_vector, bathymetry_points):
    height = solution_vector[..., 0, :, :]
    zonal_flow = solution_vector[..., 1, :, :]
    meridional = solution_vector[..., 2, :, :]
    tracers = solution_vector[..., 3:, :, :]
    zonal_new = zonal_flow[..., 1:-1] - TIME_STEP * diff_cols(height) + TIME_STEP * CORIOLIS * meridional[..., 1:-1]
    merid_new = meridional[..., 1:-1] - TIME_STEP * diff_rows(height)[..., 1:-1] - TIME_STEP * CORIOLIS * zonal_flow[..., 1:-1]
    inner_depth = bathymetry_points[..., 1:-1]
    height_new = height[..., 2:-2] - TIME_STEP * (diff_cols(inner_depth * zonal_new) + diff_rows(inner_depth * merid_new)[..., 1:-1])
    tracer_new = tracers[..., 2:-2] - TIME_STEP * (zonal_new[..., None, :, 1:-1] * diff_cols(tracers)[..., 1:-1] + merid_new[..., None, :, 1:-1] * diff_rows(tracers)[..., 2:-2])
    return jnp.concatenate([height_new[..., None, :, :], zonal_new[..., None, :, 1:-1], merid_new[..., None, :, 1:-1], tracer_new], axis=-3)


def smoothing_tables(number_of_meridional_lines, reach, number_of_lateral_lines, radius):
    row_ids = jnp.arange(number_of_meridional_lines).astype(jnp.float32)
    rows_table = jnp.maximum(0.0, 1.0 - jnp.abs(row_ids[:, None] - row_ids[None, :]) / (reach + 1.0))
    span_ids = jnp.arange(number_of_lateral_lines + 2 * radius).astype(jnp.float32)
    target_ids = jnp.arange(number_of_lateral_lines).astype(jnp.float32)
    cols_table = jnp.maximum(0.0, 1.0 - jnp.abs(span_ids[:, None] - radius - target_ids[None, :]) / (radius + 1.0))
    return rows_table, cols_table


def periodic_lateral_lines(field, extra):
    return jnp.concatenate([field[..., -extra:], field, field[..., :extra]], axis=-1)


def reference(ensemble, depth_class, obs_index, obs_value, annealing_exponents):
    bathymetry_points = 0.5 + 0.25 * depth_class.astype(jnp.float32)
    bathymetry_broadened = periodic_lateral_lines(bathymetry_points, 2)
    owner_block = jnp.arange(NOBS, dtype=jnp.int32) // OBS_DEV
    domainwide_point_number = (obs_index // COL_DEV) * COLS + owner_block * COL_DEV + obs_index % COL_DEV
    rows_table, cols_table = smoothing_tables(ROWS, ROW_REACH, COL_DEV, RADIUS)

    def ensemble_mismatch_parts(ensemble_slot):
        halfway_solution = integrate_model_ahead(periodic_lateral_lines(ensemble_slot, 2), bathymetry_broadened)
        prior_solution = integrate_model_ahead(periodic_lateral_lines(halfway_solution, 2), bathymetry_broadened)
        prognosed_solution = prior_solution[0].reshape(-1)[domainwide_point_number]
        misfit = obs_value - prognosed_solution
        loglik = jnp.zeros((ROWS * COLS,), jnp.float32).at[domainwide_point_number].add(-0.5 * misfit * misfit).reshape(ROWS, COLS)
        smoothed = jnp.dot(rows_table, loglik, precision=lax.Precision.HIGHEST)
        widened = periodic_lateral_lines(smoothed, RADIUS)
        windows = jnp.stack([widened[:, block_index * COL_DEV: block_index * COL_DEV + COL_DEV + 2 * RADIUS] for block_index in range(N_COL)])
        filtered_lateral_lines = jnp.einsum("brk,kc->rbc", windows, cols_table, precision=lax.Precision.HIGHEST).reshape(ROWS, COLS)
        return prior_solution, annealing_exponents * filtered_lateral_lines

    def absorb(running, ensemble_slot):
        peak_value, importance_aggregate, importance_scaled_solution = running
        prior_solution, logarithmic_importance = ensemble_mismatch_parts(ensemble_slot)
        revised_maximum = jnp.maximum(peak_value, logarithmic_importance)
        normalize_importance = jnp.exp(peak_value - revised_maximum)
        sample_importance = jnp.exp(logarithmic_importance - revised_maximum)
        return (revised_maximum, importance_aggregate * normalize_importance + sample_importance, importance_scaled_solution * normalize_importance[None] + sample_importance[None] * prior_solution), None

    start = (jnp.full((ROWS, COLS), -1.0e30, jnp.float32), jnp.zeros((ROWS, COLS), jnp.float32), jnp.zeros((FIELDS, ROWS, COLS), jnp.float32))
    final, unused = lax.scan(absorb, start, ensemble)
    return final[2] / final[1][None]
```

```python
import functools

import jax
import jax.numpy as jnp
from jax import lax
from jax.experimental import pallas as pl
from jax.experimental.pallas import tpu as pltpu
from jax.sharding import PartitionSpec as P

ROW_REACH = 8
TIME_STEP = 0.25
CORIOLIS = 0.2
GROUP = 16
EDGE = 4
HALF = 8
VMEM = pl.BlockSpec(memory_space=pltpu.VMEM)
ANY = pl.BlockSpec(memory_space=pl.ANY)
PARAMS = pltpu.CompilerParams(vmem_limit_bytes=56 * 1024 * 1024)
f32 = jnp.float32
bf16 = jnp.bfloat16


def depth_of(cls):
    return 0.5 + 0.25 * cls.astype(f32)


def lanes_of(shape):
    return lax.broadcasted_iota(jnp.int32, shape, len(shape) - 1)


def roll_lanes(x, shift):
    return pltpu.roll(x, shift % x.shape[-1] if isinstance(shift, int) else shift, x.ndim - 1)


def step(fields, depth, first, last):
    h, u, v, a, b = fields
    rows = h.shape[0]

    def cols(q):
        return roll_lanes(q, -1) - roll_lanes(q, 1)

    def rws(q):
        return jnp.where(last, 0.0, pltpu.roll(q, rows - 1, 0)) - jnp.where(first, 0.0, pltpu.roll(q, 1, 0))

    half = 0.5 * TIME_STEP
    un = u - half * cols(h) + TIME_STEP * CORIOLIS * v
    vn = v - half * rws(h) - TIME_STEP * CORIOLIS * u
    hn = h - half * (cols(depth * un) + rws(depth * vn))
    an = a - half * (un * cols(a) + vn * rws(a))
    bn = b - half * (un * cols(b) + vn * rws(b))
    return hn, un, vn, an, bn


def two_steps(fields, depth):
    rid = lax.broadcasted_iota(jnp.int32, depth.shape, 0)
    first, last = rid == 0, rid == depth.shape[0] - 1
    return step(step(fields, depth, first, last), depth, first, last)


def pack_kernel(x_hbm, cls_ref, idx_ref, g_ref, pa_ref, pb_ref, buf, sem):
    members, fields, rows, cols = x_hbm.shape
    per = cols // GROUP
    planes = members // per
    even = lax.rem(lax.axis_index("col"), 2) == 0
    copies = [pltpu.make_async_copy(x_hbm.at[:, f], buf.at[f], sem.at[f]) for f in range(fields)]
    for c in copies:
        c.start()

    lane = lanes_of((8, cols))
    grp = lane // GROUP
    sub = (lane % GROUP) // EDGE
    jj = lane % EDGE

    def put(plane, t, right, left):
        at = pl.ds(plane * rows + t * 8, 8)
        pa_ref[at, :] = jnp.where(even, right, left)
        pb_ref[at, :] = jnp.where(even, left, right)

    def edges(f, t):
        at = pl.ds(t * 8, 8)
        right = left = None
        for q in range(planes):
            acc = None
            for i in range(per):
                r = roll_lanes(buf[f, q * per + i, at, :], GROUP * i + HALF)
                acc = r if acc is None else jnp.where(grp == i, r, acc)
            g_ref[q, f, at, :] = acc
            r = roll_lanes(acc, EDGE * q - EDGE)
            l = roll_lanes(acc, EDGE * q - HALF)
            right = r if right is None else jnp.where(sub == q, r, right)
            left = l if left is None else jnp.where(sub == q, l, left)
        return right, left

    for f in range(3):
        copies[f].wait()

        def body(t, carry, f=f):
            right, left = edges(f, t)
            if f == 1:
                d = depth_of(cls_ref[pl.ds(t * 8, 8), :])
                for n in range(3):
                    e = roll_lanes(d, 3 * n + 3)
                    right = jnp.where(lane == EDGE * n, e, right)
                    left = jnp.where(lane == EDGE * n + 3, e, left)
            put(f, t, right, left)
            return carry

        lax.fori_loop(0, rows // 8, body, 0)
    copies[3].wait()
    copies[4].wait()

    def tracers(t, carry):
        ra, la = edges(3, t)
        rb, lb = edges(4, t)
        put(3, t, jnp.where(jj >= 2, ra, roll_lanes(rb, -2)), jnp.where(jj < 2, la, roll_lanes(lb, 2)))
        return carry

    lax.fori_loop(0, rows // 8, tracers, 0)
    n = idx_ref.shape[0]
    for ref in (pa_ref, pb_ref):
        ref[4 * rows : 4 * rows + 8, :] = jnp.zeros((8, cols), f32)
        ref[4 * rows : 4 * rows + n, :] = idx_ref[...].astype(f32)


def forecast_kernel(x_ref, cls_ref, o_ref):
    depth = depth_of(cls_ref[...])

    def body(m, carry):
        out = two_steps([x_ref[m, f] for f in range(5)], depth)
        for f in range(5):
            o_ref[m, f] = out[f]
        return carry

    lax.fori_loop(0, x_ref.shape[0], body, 0)


def pieces_of(x):
    hi = x.astype(bf16)
    rest = x - hi.astype(f32)
    mid = rest.astype(bf16)
    lo = (rest - mid.astype(f32)).astype(bf16)
    return hi, mid, lo


def row_vector(x):
    return jnp.concatenate([x[i : i + 1, :] for i in range(x.shape[0])], axis=1)


def edge_kernel(ra_ref, rb_ref, g_ref, cls_ref, x_hbm, idx_ref, obs_ref, z_ref, loss_ref, hbuf, xs, lhs, low, prod, sem):
    members, _, rows, cols = x_hbm.shape
    per = cols // GROUP
    planes = members // per
    even = lax.rem(lax.axis_index("col"), 2) == 0
    copy = pltpu.make_async_copy(x_hbm.at[:, 0], hbuf, sem)
    copy.start()
    lane = lanes_of((rows, cols))
    j = lane % GROUP
    grp = lane // GROUP

    def received(plane):
        at = slice(plane * rows, (plane + 1) * rows)
        a, b = ra_ref[at, :], rb_ref[at, :]
        return jnp.where(even, b, a), jnp.where(even, a, b)

    depth = depth_of(cls_ref[...])
    tiled = None
    for i in range(per):
        r = roll_lanes(depth, GROUP * i + HALF)
        tiled = r if tiled is None else jnp.where(grp == i, r, tiled)
    ul, ur = received(1)
    dl = roll_lanes(tiled, -EDGE)
    dr = tiled
    for n in range(3):
        dl = jnp.where(j == n + 1, jnp.broadcast_to(ul[:, EDGE * n : EDGE * n + 1], dl.shape), dl)
        dr = jnp.where(j == HALF + n, jnp.broadcast_to(ur[:, EDGE * n + 3 : EDGE * n + 4], dr.shape), dr)
    xs[0, 5] = dl
    xs[1, 5] = dr
    for f in range(5):
        left, right = received(min(f, 3))
        if f == 4:
            left, right = roll_lanes(left, 2), roll_lanes(right, -2)
        xs[0, f] = left
        xs[1, f] = right

    def strips(q, carry):
        left = []
        right = []
        for f in range(5):
            g = g_ref[q, f]
            hl = pltpu.roll(xs[0, f], lax.rem(cols - EDGE * q, cols), 1)
            hr = pltpu.roll(xs[1, f], lax.rem(cols + HALF - EDGE * q, cols), 1)
            left.append(jnp.where(j < EDGE, hl, roll_lanes(g, -EDGE)))
            right.append(jnp.where(j >= HALF, hr, g))
        left = two_steps(left, xs[0, 5])
        right = two_steps(right, xs[1, 5])
        inner = (j >= EDGE) & (j < 2 * EDGE)
        for f in range(5):
            z_ref[q, f] = jnp.where(inner, right[f], roll_lanes(left[f], EDGE))
        return carry

    lax.fori_loop(0, planes, strips, 0)

    idx = row_vector(idx_ref[...])
    obs = row_vector(obs_ref[...])
    nobs = idx.shape[1]
    row, col = lax.shift_right_logical(idx, cols.bit_length() - 1), idx & (cols - 1)
    pick = (lax.broadcasted_iota(jnp.int32, (cols, nobs), 0) == col).astype(f32).astype(bf16)
    pick2 = jnp.concatenate([pick, pick], axis=0)
    isrow = lax.broadcasted_iota(jnp.int32, (rows, nobs), 0) == row
    border = (lane < EDGE) | (lane >= cols - EDGE)
    copy.wait()

    def gather(q, carry):
        for i in range(per):
            at = slice(i * rows, (i + 1) * rows)
            h = jnp.where(border, roll_lanes(z_ref[q, 0], cols - HALF - GROUP * i), hbuf[q * per + i])
            hi, mid, lo = pieces_of(h)
            lhs[at, :cols] = hi
            lhs[at, cols:] = mid
            low[at, :] = lo
        prod[...] = jnp.dot(lhs[...], pick2, preferred_element_type=f32) + jnp.dot(
            low[...], pick, preferred_element_type=f32
        )
        ys = [
            jnp.sum(jnp.where(isrow, prod[i * rows : (i + 1) * rows, :], 0.0), axis=0, keepdims=True)
            for i in range(per)
        ]
        misfit = obs - jnp.concatenate(ys, axis=0)
        loss_ref[pl.ds(pl.multiple_of(q * per, 8), per), :] = -0.5 * misfit * misfit
        return carry

    lax.fori_loop(0, planes, gather, 0)


def spread(losses, indices, offsets, radius, cols, rows, lhs, rhs):
    members = losses[0].shape[0]
    start = 0
    for loss, idx, offset in zip(losses, indices, offsets):
        n = idx.shape[1]
        at = slice(start, start + n)
        start += n
        row, col = lax.shift_right_logical(idx, cols.bit_length() - 1), idx & (cols - 1)
        dist = jnp.abs(lax.broadcasted_iota(jnp.int32, (cols, n), 0) - (col + offset))
        table = jnp.maximum(0, radius + 1 - dist).astype(f32)
        block = lax.shift_right_logical(row, 4)
        for b in range(rows // 16):
            rhs[b * cols : (b + 1) * cols, at] = jnp.where(block == b, table, 0.0).astype(bf16)
        isrow = lax.broadcasted_iota(jnp.int32, (16, n), 0) == (row & 15)
        parts = [p.astype(f32) for p in pieces_of(loss)]
        for m in range(members):
            for p in range(3):
                lhs[p, 16 * m : 16 * m + 16, at] = jnp.where(isrow, parts[p][m : m + 1, :], 0.0).astype(bf16)
    dims = (((1,), (1,)), ((), ()))
    return sum(lax.dot_general(lhs[p], rhs[...], dims, preferred_element_type=f32) for p in range(3))


def own_kernel(loss_ref, idx_ref, o_ref, lhs, rhs, *, radius, cols, rows):
    o_ref[...] = spread([loss_ref[...]], [row_vector(idx_ref[...])], [0], radius, cols, rows, lhs, rhs)


def weigh_kernel(own_ref, la_ref, lb_ref, ra_ref, rb_ref, x_hbm, z_ref, ann_ref, *rest, radius, parts):
    outs = rest[:parts]
    lhs, rhs, acc, logw, tot, xbuf, sem = rest[parts:]
    members, fields, rows, cols = x_hbm.shape
    per = cols // GROUP
    planes = members // per
    copy = pltpu.make_async_copy(x_hbm, xbuf, sem)
    copy.start()
    even = lax.rem(lax.axis_index("col"), 2) == 0
    nrow = la_ref.shape[1] // cols
    at = slice(4 * rows, 4 * rows + nrow)
    ia = row_vector(ra_ref[at, :]).astype(jnp.int32)
    ib = row_vector(rb_ref[at, :]).astype(jnp.int32)
    oa = jnp.where(even, cols, -cols)
    acc[...] = own_ref[...] + spread(
        [la_ref[...], lb_ref[...]], [ia, ib], [oa, -oa], radius, cols, rows, lhs, rhs
    )

    pad = jnp.zeros((ROW_REACH, cols), f32)
    total_rows = rows + 2 * ROW_REACH

    def box(q, sign):
        def sh(x, s):
            return pltpu.roll(x, (total_rows - s) if sign > 0 else s, 0)

        out, width = q, 1
        while 2 * width <= ROW_REACH + 1:
            out = out + sh(out, width)
            width *= 2
        while width < ROW_REACH + 1:
            out = out + sh(q, width)
            width += 1
        return out

    scale = ann_ref[...] * (1.0 / ((ROW_REACH + 1) * (radius + 1)))

    def smooth(m, peak):
        at = pl.ds(pl.multiple_of(m * 16, 16), 16)
        q = jnp.concatenate(
            [pad] + [acc[at, b * cols : (b + 1) * cols] for b in range(rows // 16)] + [pad], axis=0
        )
        w = scale * box(box(q, 1), -1)[ROW_REACH : ROW_REACH + rows, :]
        logw[m] = w
        return jnp.maximum(peak, w)

    peak = lax.fori_loop(0, members, smooth, jnp.full((rows, cols), -jnp.inf, f32))
    tot[fields + 1] = peak
    copy.wait()
    lane = lanes_of((8, cols))
    border = (lane < EDGE) | (lane >= cols - EDGE)

    def sums(t, carry):
        at = pl.ds(pl.multiple_of(t * 8, 8), 8)
        top = tot[fields + 1, at, :]
        total = jnp.zeros((8, cols), f32)
        s = [jnp.zeros((8, cols), f32)] * fields
        for m in range(members):
            q, i = divmod(m, per)
            w = jnp.exp(logw[m, at, :] - top)
            total = total + w
            for f in range(fields):
                x = jnp.where(
                    border, roll_lanes(z_ref[q, f, at, :], cols - HALF - GROUP * i), xbuf[m, f, at, :]
                )
                s[f] = s[f] + w * x
        for f in range(fields):
            tot[f, at, :] = s[f]
        tot[fields, at, :] = total
        return carry

    lax.fori_loop(0, rows // 8, sums, 0)
    part = rows // parts
    me = lax.axis_index("dom")
    for k, ref in enumerate(outs):
        start = pl.multiple_of(partner(me, k, parts) * part, 8)
        ref[...] = tot[:, pl.ds(start, part), :]


def partner(me, k, count):
    return me ^ k if count & (count - 1) == 0 else lax.rem(me + k, count)


def swap(x, k, count):
    return lax.ppermute(x, "dom", [(i, i ^ k if count & (count - 1) == 0 else (i + k) % count) for i in range(count)])


def join_kernel(*refs):
    *ins, out = refs
    fields = out.shape[0]
    peak = functools.reduce(jnp.maximum, [r[fields + 1] for r in ins])
    total = 0.0
    s = [0.0] * fields
    for r in ins:
        e = jnp.exp(r[fields + 1] - peak)
        total = total + r[fields] * e
        for f in range(fields):
            s[f] = s[f] + r[f] * e
    for f in range(fields):
        out[f] = s[f] / total


def place_kernel(*refs):
    *ins, out = refs
    part = ins[0].shape[1]
    me = lax.axis_index("dom")
    count = len(ins)
    for k, r in enumerate(ins):
        source = me if k == 0 else (me ^ k if count & (count - 1) == 0 else lax.rem(me - k + count, count))
        out[:, pl.ds(pl.multiple_of(source * part, 8), part), :] = r[...]


def on_device(ensemble, depth_class, obs_index, obs_value, annealing_exponents):
    members, fields, rows, cols = ensemble.shape
    radius = cols // 2
    per = cols // GROUP
    planes = members // per
    nobs = obs_index.shape[0]
    ncol = lax.axis_size("col")
    ndom = lax.axis_size("dom")
    S = jax.ShapeDtypeStruct
    idx = obs_index.reshape(nobs // cols, cols)
    obs = obs_value.reshape(nobs // cols, cols)

    payload = S((4 * rows + 8, cols), f32)
    packed, pa, pb = pl.pallas_call(
        pack_kernel,
        out_shape=(S((planes, fields, rows, cols), f32), payload, payload),
        in_specs=[ANY, VMEM, VMEM],
        out_specs=(VMEM, VMEM, VMEM),
        scratch_shapes=[pltpu.VMEM((fields, members, rows, cols), f32), pltpu.SemaphoreType.DMA((fields,))],
        compiler_params=PARAMS,
        name="pack",
    )(ensemble, depth_class, idx)

    inner = [(i, i ^ 1) for i in range(ncol)]
    outer = [(i, (i + 1) % ncol if i % 2 else (i - 1) % ncol) for i in range(ncol)]

    def exchange(a, b):
        rb = lax.ppermute(b, "col", outer)
        ra = lax.ppermute(a, "col", inner)
        return ra, rb

    ra, rb = exchange(pa, pb)
    block = 4
    raw = pl.pallas_call(
        forecast_kernel,
        out_shape=S(ensemble.shape, f32),
        grid=(members // block,),
        in_specs=[
            pl.BlockSpec((block, fields, rows, cols), lambda m: (m, 0, 0, 0)),
            pl.BlockSpec((rows, cols), lambda m: (0, 0)),
        ],
        out_specs=pl.BlockSpec((block, fields, rows, cols), lambda m: (m, 0, 0, 0)),
        compiler_params=PARAMS,
        name="forecast",
    )(ensemble, depth_class)

    edges, loss = pl.pallas_call(
        edge_kernel,
        out_shape=(S((planes, fields, rows, cols), f32), S((members, nobs), f32)),
        in_specs=[VMEM, VMEM, VMEM, VMEM, ANY, VMEM, VMEM],
        out_specs=(VMEM, VMEM),
        scratch_shapes=[
            pltpu.VMEM((members, rows, cols), f32),
            pltpu.VMEM((2, fields + 1, rows, cols), f32),
            pltpu.VMEM((per * rows, 2 * cols), bf16),
            pltpu.VMEM((per * rows, cols), bf16),
            pltpu.VMEM((per * rows, nobs), f32),
            pltpu.SemaphoreType.DMA,
        ],
        compiler_params=PARAMS,
        name="edges",
    )(ra, rb, packed, depth_class, raw, idx, obs)

    la, lb = exchange(loss, loss)
    wide = rows // 16 * cols
    own = pl.pallas_call(
        functools.partial(own_kernel, radius=radius, cols=cols, rows=rows),
        out_shape=S((16 * members, wide), f32),
        in_specs=[VMEM, VMEM],
        out_specs=VMEM,
        scratch_shapes=[pltpu.VMEM((3, 16 * members, nobs), bf16), pltpu.VMEM((wide, nobs), bf16)],
        compiler_params=PARAMS,
        name="own",
    )(loss, idx)

    part = S((fields + 2, rows // ndom, cols), f32)
    sums = pl.pallas_call(
        functools.partial(weigh_kernel, radius=radius, parts=ndom),
        out_shape=(part,) * ndom,
        in_specs=[VMEM, VMEM, VMEM, VMEM, VMEM, ANY, VMEM, VMEM],
        out_specs=(VMEM,) * ndom,
        scratch_shapes=[
            pltpu.VMEM((3, 16 * members, 2 * nobs), bf16),
            pltpu.VMEM((wide, 2 * nobs), bf16),
            pltpu.VMEM((16 * members, wide), f32),
            pltpu.VMEM((members, rows, cols), f32),
            pltpu.VMEM((fields + 2, rows, cols), f32),
            pltpu.VMEM((members, fields, rows, cols), f32),
            pltpu.SemaphoreType.DMA,
        ],
        compiler_params=PARAMS,
        name="weigh",
    )(own, la, lb, ra, rb, raw, edges, annealing_exponents)

    parts = [sums[0]] + [swap(sums[k], k, ndom) for k in range(1, ndom)]
    mine = pl.pallas_call(
        join_kernel,
        out_shape=S((fields, rows // ndom, cols), f32),
        in_specs=[VMEM] * ndom,
        out_specs=VMEM,
        compiler_params=PARAMS,
        name="join",
    )(*parts)
    blocks = [mine] + [swap(mine, k, ndom) for k in range(1, ndom)]
    return pl.pallas_call(
        place_kernel,
        out_shape=S((fields, rows, cols), f32),
        in_specs=[VMEM] * ndom,
        out_specs=VMEM,
        compiler_params=PARAMS,
        name="place",
    )(*blocks)


def solution(mesh):
    in_specs = (P("dom", None, None, "col"), P(None, "col"), P("col"), P("col"), P(None, "col"))
    out_specs = P(None, None, "col")
    return jax.shard_map(
        on_device, mesh=mesh, in_specs=in_specs, out_specs=out_specs, check_vma=False
    )
```

```python
import functools

import jax
import jax.numpy as jnp
from jax import lax
from jax.experimental import pallas as pl
from jax.experimental.pallas import tpu as pltpu
from jax.sharding import PartitionSpec as P

ROW_REACH = 8
TIME_STEP = 0.25
CORIOLIS = 0.2
GROUP = 16
EDGE = 4
ZEROS = 8
BANDS = 4
HALF = 8
f32 = jnp.float32
bf16 = jnp.bfloat16
VMEM = pl.BlockSpec(memory_space=pltpu.VMEM)
HBM = pl.BlockSpec(memory_space=pltpu.HBM)


def params(mib):
    return pltpu.CompilerParams(vmem_limit_bytes=mib * 1024 * 1024)


def depth_of(cls):
    return 0.5 + 0.25 * cls.astype(f32)


def lanes_of(shape):
    return lax.broadcasted_iota(jnp.int32, shape, len(shape) - 1)


def roll_lanes(x, shift):
    return pltpu.roll(x, shift % x.shape[-1] if isinstance(shift, int) else shift, x.ndim - 1)


def shift_table(cols):
    k = lax.broadcasted_iota(jnp.int32, (2 * cols, cols), 0) & (cols - 1)
    c = lax.broadcasted_iota(jnp.int32, (2 * cols, cols), 1)
    return (jnp.where(k == c + 1, 1.0, 0.0) - jnp.where(k == c - 1, 1.0, 0.0)).astype(bf16)


def step(fields, depth, pad, slot, table):
    h, u, v, a, b = fields
    rows = h.shape[0]

    def cols(q):
        return roll_lanes(q, -1) - roll_lanes(q, 1)

    def rws(q, n):
        pad[slot + n, ZEROS : ZEROS + rows, :] = q
        return pad[slot + n, ZEROS + 1 : ZEROS + 1 + rows, :] - pad[slot + n, ZEROS - 1 : ZEROS - 1 + rows, :]

    both = jnp.concatenate([a, b], axis=0)
    hi = both.astype(bf16)
    mid = (both - hi.astype(f32)).astype(bf16)
    slopes = jnp.dot(jnp.concatenate([hi, mid], axis=1), table[...], preferred_element_type=f32)
    half = 0.5 * TIME_STEP
    un = u - half * cols(h) + TIME_STEP * CORIOLIS * v
    vn = v - half * rws(h, 0) - TIME_STEP * CORIOLIS * u
    hn = h - half * (cols(depth * un) + rws(depth * vn, 1))
    an = a - half * (un * slopes[:rows] + vn * rws(a, 2))
    bn = b - half * (un * slopes[rows:] + vn * rws(b, 3))
    return hn, un, vn, an, bn


def prepare(pad, table):
    for n in range(pad.shape[0]):
        pad[n, :ZEROS, :] = jnp.zeros((ZEROS, pad.shape[2]), f32)
        pad[n, pad.shape[1] - ZEROS :, :] = jnp.zeros((ZEROS, pad.shape[2]), f32)
    table[...] = shift_table(table.shape[1])


def two_steps(fields, depth, pad, table, slot=0):
    return step(step(fields, depth, pad, slot, table), depth, pad, slot + 4, table)


def pack_kernel(x_hbm, cls_ref, idx_ref, g_ref, pa_ref, pb_ref, buf, sem):
    members, fields, rows, cols = x_hbm.shape
    per = cols // GROUP
    planes = members // per
    even = lax.rem(lax.axis_index("col"), 2) == 0
    copies = [pltpu.make_async_copy(x_hbm.at[:, f], buf.at[f], sem.at[f]) for f in range(fields)]
    for c in copies:
        c.start()

    lane = lanes_of((8, cols))
    grp = lane // GROUP
    sub = (lane % GROUP) // EDGE
    jj = lane % EDGE

    def put(plane, t, right, left):
        at = pl.ds(plane * rows + t * 8, 8)
        pa_ref[at, :] = jnp.where(even, right, left)
        pb_ref[at, :] = jnp.where(even, left, right)

    def edges(f, t):
        at = pl.ds(t * 8, 8)
        right = left = None
        for q in range(planes):
            acc = None
            for i in range(per):
                r = roll_lanes(buf[f, q * per + i, at, :], GROUP * i + HALF)
                acc = r if acc is None else jnp.where(grp == i, r, acc)
            g_ref[q, f, at, :] = acc
            r = roll_lanes(acc, EDGE * q - EDGE)
            l = roll_lanes(acc, EDGE * q - HALF)
            right = r if right is None else jnp.where(sub == q, r, right)
            left = l if left is None else jnp.where(sub == q, l, left)
        return right, left

    for f in range(3):
        copies[f].wait()

        def body(t, carry, f=f):
            right, left = edges(f, t)
            if f == 1:
                d = depth_of(cls_ref[pl.ds(t * 8, 8), :])
                for n in range(3):
                    e = roll_lanes(d, 3 * n + 3)
                    right = jnp.where(lane == EDGE * n, e, right)
                    left = jnp.where(lane == EDGE * n + 3, e, left)
            put(f, t, right, left)
            return carry

        lax.fori_loop(0, rows // 8, body, 0, unroll=4)
    copies[3].wait()
    copies[4].wait()

    def tracers(t, carry):
        ra, la = edges(3, t)
        rb, lb = edges(4, t)
        put(3, t, jnp.where(jj >= 2, ra, roll_lanes(rb, -2)), jnp.where(jj < 2, la, roll_lanes(lb, 2)))
        return carry

    lax.fori_loop(0, rows // 8, tracers, 0, unroll=2)
    n = idx_ref.shape[0]
    for ref in (pa_ref, pb_ref):
        ref[4 * rows : 4 * rows + 8, :] = jnp.zeros((8, cols), f32)
        ref[4 * rows : 4 * rows + n, :] = idx_ref[...].astype(f32)


def forecast_kernel(x_ref, cls_ref, o_ref, pad, table):
    depth = depth_of(cls_ref[...])
    pl.when(pl.program_id(0) == 0)(lambda: prepare(pad, table))

    def body(m, carry):
        out = two_steps([x_ref[m, f] for f in range(5)], depth, pad, table)
        for f in range(5):
            o_ref[m, f] = out[f]
        return carry

    lax.fori_loop(0, x_ref.shape[0], body, 0, unroll=4)


def pieces_of(x):
    hi = x.astype(bf16)
    rest = x - hi.astype(f32)
    mid = rest.astype(bf16)
    lo = (rest - mid.astype(f32)).astype(bf16)
    return hi, mid, lo


def row_vector(x):
    return jnp.concatenate([x[i : i + 1, :] for i in range(x.shape[0])], axis=1)


def edge_kernel(ra_ref, rb_ref, g_ref, cls_ref, x_ref, idx_ref, obs_ref, z_ref, loss_ref, xs, pad, table, lhs, low, prod):
    members, _, rows, cols = x_ref.shape
    per = cols // GROUP
    planes = members // per
    even = lax.rem(lax.axis_index("col"), 2) == 0
    lane = lanes_of((rows, cols))
    j = lane % GROUP
    grp = lane // GROUP

    def received(plane):
        at = slice(plane * rows, (plane + 1) * rows)
        a, b = ra_ref[at, :], rb_ref[at, :]
        return jnp.where(even, b, a), jnp.where(even, a, b)

    depth = depth_of(cls_ref[...])
    tiled = None
    for i in range(per):
        r = roll_lanes(depth, GROUP * i + HALF)
        tiled = r if tiled is None else jnp.where(grp == i, r, tiled)
    ul, ur = received(1)
    dl = roll_lanes(tiled, -EDGE)
    dr = tiled
    for n in range(3):
        dl = jnp.where(j == n + 1, jnp.broadcast_to(ul[:, EDGE * n : EDGE * n + 1], dl.shape), dl)
        dr = jnp.where(j == HALF + n, jnp.broadcast_to(ur[:, EDGE * n + 3 : EDGE * n + 4], dr.shape), dr)
    xs[0, 5] = dl
    xs[1, 5] = dr
    for f in range(5):
        left, right = received(min(f, 3))
        if f == 4:
            left, right = roll_lanes(left, 2), roll_lanes(right, -2)
        xs[0, f] = left
        xs[1, f] = right

    def strips(q, carry):
        left = []
        right = []
        for f in range(5):
            g = g_ref[q, f]
            hl = pltpu.roll(xs[0, f], lax.rem(cols - EDGE * q, cols), 1)
            hr = pltpu.roll(xs[1, f], lax.rem(cols + HALF - EDGE * q, cols), 1)
            left.append(jnp.where(j < EDGE, hl, roll_lanes(g, -EDGE)))
            right.append(jnp.where(j >= HALF, hr, g))
        left = two_steps(left, xs[0, 5], pad, table)
        right = two_steps(right, xs[1, 5], pad, table, 8)
        inner = (j >= EDGE) & (j < 2 * EDGE)
        for f in range(5):
            z_ref[q, f] = jnp.where(inner, right[f], roll_lanes(left[f], EDGE))
        return carry

    prepare(pad, table)
    lax.fori_loop(0, planes, strips, 0)

    idx = row_vector(idx_ref[...])
    obs = row_vector(obs_ref[...])
    nobs = idx.shape[1]
    row, col = lax.shift_right_logical(idx, cols.bit_length() - 1), idx & (cols - 1)
    pick = (lax.broadcasted_iota(jnp.int32, (cols, nobs), 0) == col).astype(f32).astype(bf16)
    pick2 = jnp.concatenate([pick, pick], axis=0)
    isrow = lax.broadcasted_iota(jnp.int32, (rows, nobs), 0) == row
    border = (lane < EDGE) | (lane >= cols - EDGE)

    def gather(q, carry):
        for i in range(per):
            at = slice(i * rows, (i + 1) * rows)
            h = jnp.where(border, roll_lanes(z_ref[q, 0], cols - HALF - GROUP * i), x_ref[q * per + i, 0])
            hi, mid, lo = pieces_of(h)
            lhs[at, :cols] = hi
            lhs[at, cols:] = mid
            low[at, :] = lo
        prod[...] = jnp.dot(lhs[...], pick2, preferred_element_type=f32) + jnp.dot(
            low[...], pick, preferred_element_type=f32
        )
        ys = [
            jnp.sum(jnp.where(isrow, prod[i * rows : (i + 1) * rows, :], 0.0), axis=0, keepdims=True)
            for i in range(per)
        ]
        misfit = obs - jnp.concatenate(ys, axis=0)
        loss_ref[pl.ds(pl.multiple_of(q * per, 8), per), :] = -0.5 * misfit * misfit
        return carry

    lax.fori_loop(0, planes, gather, 0)


def spread(loss, idx, offset, first, width, order, radius, cols, rows, lhs, rhs):
    members, n = loss.shape
    band = rows // BANDS
    col = idx & (cols - 1)
    row = lax.shift_right_logical(idx, cols.bit_length() - 1)
    dist = jnp.abs(lax.broadcasted_iota(jnp.int32, (width, n), 0) + (first - offset) - col)
    table = jnp.maximum(0, radius + 1 - dist).astype(f32)
    block = sum(jnp.where(row >= band * b, 1, 0) for b in range(1, BANDS))
    for pos, b in enumerate(order):
        rhs[pos * width : (pos + 1) * width, :] = jnp.where(block == b, table, 0.0).astype(bf16)
    isrow = lax.broadcasted_iota(jnp.int32, (band, n), 0) == row - band * block
    for p, part in enumerate(pieces_of(loss)):
        part = part.astype(f32)
        for m in range(0, members, 2):
            pair = [jnp.where(isrow, part[m + i : m + i + 1, :], 0.0) for i in range(2)]
            lhs[p, band * m : band * (m + 2), :] = jnp.concatenate(pair, axis=0).astype(bf16)
    dims = (((1,), (1,)), ((), ()))
    return sum(lax.dot_general(lhs[p], rhs[...], dims, preferred_element_type=f32) for p in range(3))


def own_kernel(loss_ref, idx_ref, o_ref, lhs, rhs, *, radius, cols, rows):
    o_ref[...] = spread(
        loss_ref[...], row_vector(idx_ref[...]), 0, 0, cols, range(BANDS), radius, cols, rows, lhs, rhs
    )


def triangle(q, bufs):
    rows = q.shape[0]
    size = rows + 2 * ROW_REACH
    low = 2 * ZEROS
    bufs[0, low : low + rows, :] = q
    start, count = ZEROS, size
    for n, gap in enumerate((1, 3, 1, 3)):
        if n == 3:
            start, count = low, rows
        y = (
            bufs[n, start - gap : start - gap + count, :]
            + bufs[n, start : start + count, :]
            + bufs[n, start + gap : start + gap + count, :]
        )
        if n < 3:
            bufs[n + 1, start : start + count, :] = y
    return y


def weigh_kernel(own_ref, la_ref, lb_ref, ra_ref, rb_ref, x_ref, z_ref, ann_ref, *rest, radius, parts):
    outs = rest[:parts]
    lhs, rhs, near, logw, tot, bufs = rest[parts:]
    members, fields, rows, cols = x_ref.shape
    per = cols // GROUP
    planes = members // per
    band = rows // BANDS
    even = lax.rem(lax.axis_index("col"), 2) == 0
    nrow = la_ref.shape[1] // cols
    at = slice(4 * rows, 4 * rows + nrow)
    ia = row_vector(ra_ref[at, :]).astype(jnp.int32)
    ib = row_vector(rb_ref[at, :]).astype(jnp.int32)
    left = jnp.where(even, lb_ref[...], la_ref[...])
    right = jnp.where(even, la_ref[...], lb_ref[...])
    mid = cols // 2
    swapped = [b ^ 1 for b in range(BANDS)]
    near[0] = spread(
        left, jnp.where(even, ib, ia), -cols, 0, mid, range(BANDS), radius, cols, rows, lhs.at[0], rhs.at[0]
    )
    near[1] = spread(
        right, jnp.where(even, ia, ib), cols, mid, mid, swapped, radius, cols, rows, lhs.at[1], rhs.at[1]
    )
    for n in range(bufs.shape[0]):
        for k in range(4):
            bufs[n, k, : 2 * ZEROS, :] = jnp.zeros((2 * ZEROS, cols), f32)
            bufs[n, k, rows + 2 * ZEROS :, :] = jnp.zeros((2 * ZEROS, cols), f32)

    scale = ann_ref[...] * (1.0 / ((ROW_REACH + 1) * (radius + 1)))
    lower = lanes_of((band, cols)) < mid

    def smooth(g, peak):
        for n in range(bufs.shape[0]):
            m = g * bufs.shape[0] + n
            at = pl.ds(pl.multiple_of(m * band, 8), band)
            q = []
            for b in range(0, BANDS, 2):
                l = near[0, at, b * mid : (b + 2) * mid]
                r = near[1, at, b * mid : (b + 2) * mid]
                q.append(own_ref[at, b * cols : (b + 1) * cols] + jnp.where(lower, l, r))
                q.append(
                    own_ref[at, (b + 1) * cols : (b + 2) * cols] + roll_lanes(jnp.where(lower, r, l), mid)
                )
            w = scale * triangle(jnp.concatenate(q, axis=0), bufs.at[n])
            logw[m] = w
            peak = jnp.maximum(peak, w)
        return peak

    peak = lax.fori_loop(0, members // bufs.shape[0], smooth, jnp.full((rows, cols), -jnp.inf, f32))
    tot[fields + 1] = peak
    lane = lanes_of((8, cols))
    grp = lane // GROUP
    border = (lane < EDGE) | (lane >= cols - EDGE)

    def sums(t, carry):
        at = pl.ds(pl.multiple_of(t * 8, 8), 8)
        top = tot[fields + 1, at, :]
        total = jnp.zeros((8, cols), f32)
        s = [jnp.zeros((8, cols), f32)] * fields
        e = [jnp.zeros((8, cols), f32)] * fields
        for q in range(planes):
            packed = None
            for i in range(per):
                m = q * per + i
                w = jnp.exp(logw[m, at, :] - top)
                total = total + w
                for f in range(fields):
                    s[f] = s[f] + w * x_ref[m, f, at, :]
                r = roll_lanes(w, GROUP * i + HALF)
                packed = r if packed is None else jnp.where(grp == i, r, packed)
            for f in range(fields):
                e[f] = e[f] + packed * z_ref[q, f, at, :]
        for f in range(fields):
            for k in (cols // 2, cols // 4, cols // 8):
                e[f] = e[f] + roll_lanes(e[f], k)
            tot[f, at, :] = jnp.where(border, roll_lanes(e[f], cols - HALF), s[f])
        tot[fields, at, :] = total
        return carry

    lax.fori_loop(0, rows // 8, sums, 0)
    part = rows // parts
    me = lax.axis_index("dom")
    for k, ref in enumerate(outs):
        start = pl.multiple_of(partner(me, k, parts) * part, 8)
        ref[...] = tot[:, pl.ds(start, part), :]


def partner(me, k, count):
    return me ^ k if count & (count - 1) == 0 else lax.rem(me + k, count)


def swap(x, k, count):
    return lax.ppermute(x, "dom", [(i, i ^ k if count & (count - 1) == 0 else (i + k) % count) for i in range(count)])


def join_kernel(*refs):
    *ins, out = refs
    fields = out.shape[0]
    peak = functools.reduce(jnp.maximum, [r[fields + 1] for r in ins])
    total = 0.0
    s = [0.0] * fields
    for r in ins:
        e = jnp.exp(r[fields + 1] - peak)
        total = total + r[fields] * e
        for f in range(fields):
            s[f] = s[f] + r[f] * e
    for f in range(fields):
        out[f] = s[f] / total


def place_kernel(*refs):
    *ins, out = refs
    part = ins[0].shape[1]
    me = lax.axis_index("dom")
    count = len(ins)
    for k, r in enumerate(ins):
        source = me if k == 0 else (me ^ k if count & (count - 1) == 0 else lax.rem(me - k + count, count))
        out[:, pl.ds(pl.multiple_of(source * part, 8), part), :] = r[...]


def on_device(ensemble, depth_class, obs_index, obs_value, annealing_exponents):
    members, fields, rows, cols = ensemble.shape
    radius = cols // 2
    per = cols // GROUP
    planes = members // per
    nobs = obs_index.shape[0]
    ncol = lax.axis_size("col")
    ndom = lax.axis_size("dom")
    S = jax.ShapeDtypeStruct
    idx = obs_index.reshape(nobs // cols, cols)
    obs = obs_value.reshape(nobs // cols, cols)

    payload = S((4 * rows + 8, cols), f32)
    packed, pa, pb = pl.pallas_call(
        pack_kernel,
        out_shape=(S((planes, fields, rows, cols), f32), payload, payload),
        in_specs=[HBM, VMEM, VMEM],
        out_specs=(VMEM, VMEM, VMEM),
        scratch_shapes=[pltpu.VMEM((fields, members, rows, cols), f32), pltpu.SemaphoreType.DMA((fields,))],
        compiler_params=params(14),
        name="pack",
    )(ensemble, depth_class, idx)

    inner = [(i, i ^ 1) for i in range(ncol)]
    outer = [(i, (i + 1) % ncol if i % 2 else (i - 1) % ncol) for i in range(ncol)]

    def exchange(a, b):
        rb = lax.ppermute(b, "col", outer)
        ra = lax.ppermute(a, "col", inner)
        return ra, rb

    ra, rb = exchange(pa, pb)
    block = 4
    raw = pl.pallas_call(
        forecast_kernel,
        out_shape=S(ensemble.shape, f32),
        grid=(members // block,),
        in_specs=[
            pl.BlockSpec((block, fields, rows, cols), lambda m: (m, 0, 0, 0)),
            pl.BlockSpec((rows, cols), lambda m: (0, 0)),
        ],
        out_specs=pl.BlockSpec((block, fields, rows, cols), lambda m: (m, 0, 0, 0)),
        scratch_shapes=[pltpu.VMEM((8, rows + 2 * ZEROS, cols), f32), pltpu.VMEM((2 * cols, cols), bf16)],
        compiler_params=params(12),
        name="forecast",
    )(ensemble, depth_class)

    edges, loss = pl.pallas_call(
        edge_kernel,
        out_shape=(S((planes, fields, rows, cols), f32), S((members, nobs), f32)),
        in_specs=[VMEM] * 7,
        out_specs=(VMEM, VMEM),
        scratch_shapes=[
            pltpu.VMEM((2, fields + 1, rows, cols), f32),
            pltpu.VMEM((16, rows + 2 * ZEROS, cols), f32),
            pltpu.VMEM((2 * cols, cols), bf16),
            pltpu.VMEM((per * rows, 2 * cols), bf16),
            pltpu.VMEM((per * rows, cols), bf16),
            pltpu.VMEM((per * rows, nobs), f32),
        ],
        compiler_params=params(18),
        name="edges",
    )(ra, rb, packed, depth_class, raw, idx, obs)

    la, lb = exchange(loss, loss)
    tall = members * rows // BANDS
    own = pl.pallas_call(
        functools.partial(own_kernel, radius=radius, cols=cols, rows=rows),
        out_shape=S((tall, BANDS * cols), f32),
        in_specs=[VMEM, VMEM],
        out_specs=VMEM,
        scratch_shapes=[pltpu.VMEM((3, tall, nobs), bf16), pltpu.VMEM((BANDS * cols, nobs), bf16)],
        compiler_params=params(10),
        name="own",
    )(loss, idx)

    part = S((fields + 2, rows // ndom, cols), f32)
    sums = pl.pallas_call(
        functools.partial(weigh_kernel, radius=radius, parts=ndom),
        out_shape=(part,) * ndom,
        in_specs=[VMEM] * 8,
        out_specs=(VMEM,) * ndom,
        scratch_shapes=[
            pltpu.VMEM((2, 3, tall, nobs), bf16),
            pltpu.VMEM((2, BANDS * cols // 2, nobs), bf16),
            pltpu.VMEM((2, tall, BANDS * cols // 2), f32),
            pltpu.VMEM((members, rows, cols), f32),
            pltpu.VMEM((fields + 2, rows, cols), f32),
            pltpu.VMEM((2, 4, rows + 4 * ZEROS, cols), f32),
        ],
        compiler_params=params(30),
        name="weigh",
    )(own, la, lb, ra, rb, raw, edges, annealing_exponents)

    parts = [sums[0]] + [swap(sums[k], k, ndom) for k in range(1, ndom)]
    mine = pl.pallas_call(
        join_kernel,
        out_shape=S((fields, rows // ndom, cols), f32),
        in_specs=[VMEM] * ndom,
        out_specs=VMEM,
        compiler_params=params(4),
        name="join",
    )(*parts)
    blocks = [mine] + [swap(mine, k, ndom) for k in range(1, ndom)]
    return pl.pallas_call(
        place_kernel,
        out_shape=S((fields, rows, cols), f32),
        in_specs=[VMEM] * ndom,
        out_specs=VMEM,
        compiler_params=params(4),
        name="place",
    )(*blocks)


def solution(mesh):
    in_specs = (P("dom", None, None, "col"), P(None, "col"), P("col"), P("col"), P(None, "col"))
    out_specs = P(None, None, "col")
    return jax.shard_map(
        on_device, mesh=mesh, in_specs=in_specs, out_specs=out_specs, check_vma=False
    )
```

```python
import functools

import jax
import jax.numpy as jnp
from jax import lax
from jax.experimental import pallas as pl
from jax.experimental.pallas import tpu as pltpu
from jax.sharding import PartitionSpec as P

ROW_REACH = 8
TIME_STEP = 0.25
CORIOLIS = 0.2
GROUP = 16
EDGE = 4
ZEROS = 8
BANDS = 4
HALF = 8
f32 = jnp.float32
bf16 = jnp.bfloat16
VMEM = pl.BlockSpec(memory_space=pltpu.VMEM)
HBM = pl.BlockSpec(memory_space=pltpu.HBM)


def params(mib):
    return pltpu.CompilerParams(vmem_limit_bytes=mib * 1024 * 1024)


def depth_of(cls):
    return 0.5 + 0.25 * cls.astype(f32)


def lanes_of(shape):
    return lax.broadcasted_iota(jnp.int32, shape, len(shape) - 1)


def roll_lanes(x, shift):
    return pltpu.roll(x, shift % x.shape[-1] if isinstance(shift, int) else shift, x.ndim - 1)


def shift_table(cols):
    k = lax.broadcasted_iota(jnp.int32, (2 * cols, cols), 0) & (cols - 1)
    c = lax.broadcasted_iota(jnp.int32, (2 * cols, cols), 1)
    return (jnp.where(k == c + 1, 1.0, 0.0) - jnp.where(k == c - 1, 1.0, 0.0)).astype(bf16)


def step(fields, depth, pad, slot, table):
    h, u, v, a, b = fields
    rows = h.shape[0]

    def cols(q):
        return roll_lanes(q, -1) - roll_lanes(q, 1)

    def rws(q, n):
        pad[slot + n, ZEROS : ZEROS + rows, :] = q
        return pad[slot + n, ZEROS + 1 : ZEROS + 1 + rows, :] - pad[slot + n, ZEROS - 1 : ZEROS - 1 + rows, :]

    both = jnp.concatenate([a, b], axis=0)
    hi = both.astype(bf16)
    mid = (both - hi.astype(f32)).astype(bf16)
    slopes = jnp.dot(jnp.concatenate([hi, mid], axis=1), table[...], preferred_element_type=f32)
    half = 0.5 * TIME_STEP
    un = u - half * cols(h) + TIME_STEP * CORIOLIS * v
    vn = v - half * rws(h, 0) - TIME_STEP * CORIOLIS * u
    hn = h - half * (cols(depth * un) + rws(depth * vn, 1))
    an = a - half * (un * slopes[:rows] + vn * rws(a, 2))
    bn = b - half * (un * slopes[rows:] + vn * rws(b, 3))
    return hn, un, vn, an, bn


def prepare(pad, table):
    for n in range(pad.shape[0]):
        pad[n, :ZEROS, :] = jnp.zeros((ZEROS, pad.shape[2]), f32)
        pad[n, pad.shape[1] - ZEROS :, :] = jnp.zeros((ZEROS, pad.shape[2]), f32)
    table[...] = shift_table(table.shape[1])


def two_steps(fields, depth, pad, table, slot=0):
    return step(step(fields, depth, pad, slot, table), depth, pad, slot + 4, table)


def pack_kernel(x_hbm, cls_hbm, idx_hbm, g_ref, pa_ref, pb_ref, buf, cls_ref, idx_ref, sem):
    members, fields, rows, cols = x_hbm.shape
    per = cols // GROUP
    planes = members // per
    even = lax.rem(lax.axis_index("col"), 2) == 0
    copies = [pltpu.make_async_copy(x_hbm.at[:, f], buf.at[f], sem.at[f]) for f in range(fields)]
    copies.append(pltpu.make_async_copy(cls_hbm, cls_ref, sem.at[fields]))
    copies.append(pltpu.make_async_copy(idx_hbm, idx_ref, sem.at[fields + 1]))
    for c in copies:
        c.start()

    lane = lanes_of((8, cols))
    grp = lane // GROUP
    sub = (lane % GROUP) // EDGE
    jj = lane % EDGE

    def put(plane, t, right, left):
        at = pl.ds(plane * rows + t * 8, 8)
        pa_ref[at, :] = jnp.where(even, right, left)
        pb_ref[at, :] = jnp.where(even, left, right)

    def edges(f, t):
        at = pl.ds(t * 8, 8)
        right = left = None
        for q in range(planes):
            acc = None
            for i in range(per):
                r = roll_lanes(buf[f, q * per + i, at, :], GROUP * i + HALF)
                acc = r if acc is None else jnp.where(grp == i, r, acc)
            g_ref[q, f, at, :] = acc
            r = roll_lanes(acc, EDGE * q - EDGE)
            l = roll_lanes(acc, EDGE * q - HALF)
            right = r if right is None else jnp.where(sub == q, r, right)
            left = l if left is None else jnp.where(sub == q, l, left)
        return right, left

    for f in range(3):
        copies[f].wait()
        if f == 1:
            copies[fields].wait()

        def body(t, carry, f=f):
            right, left = edges(f, t)
            if f == 1:
                d = depth_of(cls_ref[pl.ds(t * 8, 8), :])
                for n in range(3):
                    e = roll_lanes(d, 3 * n + 3)
                    right = jnp.where(lane == EDGE * n, e, right)
                    left = jnp.where(lane == EDGE * n + 3, e, left)
            put(f, t, right, left)
            return carry

        lax.fori_loop(0, rows // 8, body, 0, unroll=4)
    copies[3].wait()
    copies[4].wait()

    def tracers(t, carry):
        ra, la = edges(3, t)
        rb, lb = edges(4, t)
        put(3, t, jnp.where(jj >= 2, ra, roll_lanes(rb, -2)), jnp.where(jj < 2, la, roll_lanes(lb, 2)))
        return carry

    lax.fori_loop(0, rows // 8, tracers, 0, unroll=2)
    copies[fields + 1].wait()
    n = idx_ref.shape[0]
    for ref in (pa_ref, pb_ref):
        ref[4 * rows : 4 * rows + 8, :] = jnp.zeros((8, cols), f32)
        ref[4 * rows : 4 * rows + n, :] = idx_ref[...].astype(f32)


def forecast_kernel(x_ref, cls_ref, o_ref, pad, table):
    depth = depth_of(cls_ref[...])
    pl.when(pl.program_id(0) == 0)(lambda: prepare(pad, table))

    def body(m, carry):
        out = two_steps([x_ref[f, m] for f in range(5)], depth, pad, table)
        for f in range(5):
            o_ref[m, f] = out[f]
        return carry

    lax.fori_loop(0, o_ref.shape[0], body, 0, unroll=4)


def pieces_of(x):
    hi = x.astype(bf16)
    rest = x - hi.astype(f32)
    mid = rest.astype(bf16)
    lo = (rest - mid.astype(f32)).astype(bf16)
    return hi, mid, lo


def row_vector(x):
    return jnp.concatenate([x[i : i + 1, :] for i in range(x.shape[0])], axis=1)


def edge_kernel(ra_ref, rb_ref, g_ref, cls_ref, x_ref, idx_ref, obs_ref, z_ref, loss_ref, xs, pad, table, lhs, pick, prod):
    members, _, rows, cols = x_ref.shape
    per = cols // GROUP
    planes = members // per
    even = lax.rem(lax.axis_index("col"), 2) == 0
    lane = lanes_of((rows, cols))
    j = lane % GROUP
    grp = lane // GROUP

    def received(plane):
        at = slice(plane * rows, (plane + 1) * rows)
        a, b = ra_ref[at, :], rb_ref[at, :]
        return jnp.where(even, b, a), jnp.where(even, a, b)

    depth = depth_of(cls_ref[...])
    tiled = None
    for i in range(per):
        r = roll_lanes(depth, GROUP * i + HALF)
        tiled = r if tiled is None else jnp.where(grp == i, r, tiled)
    ul, ur = received(1)
    dl = dr = tiled
    for n in range(3):
        dl = jnp.where(j == EDGE + n + 1, jnp.broadcast_to(ul[:, EDGE * n : EDGE * n + 1], dl.shape), dl)
        dr = jnp.where(j == HALF + n, jnp.broadcast_to(ur[:, EDGE * n + 3 : EDGE * n + 4], dr.shape), dr)
    xs[0, 5] = dl
    xs[1, 5] = dr
    for f in range(5):
        left, right = received(min(f, 3))
        if f == 4:
            left, right = roll_lanes(left, 2), roll_lanes(right, -2)
        xs[0, f] = left
        xs[1, f] = right

    def strips(q, carry):
        left = []
        right = []
        for f in range(5):
            g = g_ref[q, f]
            hl = pltpu.roll(xs[0, f], lax.rem(cols + EDGE - EDGE * q, cols), 1)
            hr = pltpu.roll(xs[1, f], lax.rem(cols + HALF - EDGE * q, cols), 1)
            left.append(jnp.where((j >= EDGE) & (j < HALF), hl, g))
            right.append(jnp.where(j >= HALF, hr, g))
        left = two_steps(left, xs[0, 5], pad, table)
        right = two_steps(right, xs[1, 5], pad, table, 8)
        for f in range(5):
            z_ref[q, f] = jnp.where(j < HALF, right[f], left[f])
        return carry

    prepare(pad, table)
    lax.fori_loop(0, planes, strips, 0)

    idx = row_vector(idx_ref[...])
    obs = row_vector(obs_ref[...])
    nobs = idx.shape[1]
    row, col = lax.shift_right_logical(idx, cols.bit_length() - 1), idx & (cols - 1)
    band = rows // BANDS
    block = sum(jnp.where(row >= band * b, 1, 0) for b in range(1, BANDS))
    here = lax.broadcasted_iota(jnp.int32, (cols, nobs), 0) == col
    for b in range(BANDS):
        pick[b * cols : (b + 1) * cols, :] = jnp.where(here & (block == b), 1.0, 0.0).astype(bf16)
    isrow = lax.broadcasted_iota(jnp.int32, (band, nobs), 0) == row - band * block
    border = (lane < EDGE) | (lane >= cols - EDGE)

    def split(q, carry):
        for i in range(0, per, 2):
            pair = [
                jnp.where(border, roll_lanes(z_ref[q, 0], cols - HALF - GROUP * n), x_ref[q * per + n, 0])
                for n in (i, i + 1)
            ]
            at = pl.ds(pl.multiple_of((q * per + i) * band, 16), 2 * band)
            for b in range(BANDS):
                both = jnp.concatenate([h[b * band : (b + 1) * band] for h in pair], axis=0)
                for p, piece in enumerate(pieces_of(both)):
                    lhs[p, at, b * cols : (b + 1) * cols] = piece
        return carry

    lax.fori_loop(0, planes, split, 0)
    prod[...] = sum(jnp.dot(lhs[p], pick[...], preferred_element_type=f32) for p in range(3))

    def gather(q, carry):
        ys = []
        for i in range(per):
            at = pl.ds(pl.multiple_of((q * per + i) * band, 8), band)
            ys.append(jnp.sum(jnp.where(isrow, prod[at, :], 0.0), axis=0, keepdims=True))
        misfit = obs - jnp.concatenate(ys, axis=0)
        loss_ref[pl.ds(pl.multiple_of(q * per, 8), per), :] = -0.5 * misfit * misfit
        return carry

    lax.fori_loop(0, planes, gather, 0)


def spread(loss, idx, offset, first, width, order, radius, cols, rows, lhs, rhs):
    members, n = loss.shape
    band = rows // BANDS
    col = idx & (cols - 1)
    row = lax.shift_right_logical(idx, cols.bit_length() - 1)
    dist = jnp.abs(lax.broadcasted_iota(jnp.int32, (width, n), 0) + (first - offset) - col)
    table = jnp.maximum(0, radius + 1 - dist).astype(f32)
    block = sum(jnp.where(row >= band * b, 1, 0) for b in range(1, BANDS))
    for pos, b in enumerate(order):
        rhs[pos * width : (pos + 1) * width, :] = jnp.where(block == b, table, 0.0).astype(bf16)
    isrow = lax.broadcasted_iota(jnp.int32, (band, n), 0) == row - band * block
    for p, part in enumerate(pieces_of(loss)):
        part = part.astype(f32)
        for m in range(0, members, 2):
            pair = [jnp.where(isrow, part[m + i : m + i + 1, :], 0.0) for i in range(2)]
            lhs[p, band * m : band * (m + 2), :] = jnp.concatenate(pair, axis=0).astype(bf16)
    dims = (((1,), (1,)), ((), ()))
    return sum(lax.dot_general(lhs[p], rhs[...], dims, preferred_element_type=f32) for p in range(3))


def own_kernel(loss_ref, idx_ref, o_ref, lhs, rhs, *, radius, cols, rows):
    o_ref[...] = spread(
        loss_ref[...], row_vector(idx_ref[...]), 0, 0, cols, range(BANDS), radius, cols, rows, lhs, rhs
    )


def triangle(q, bufs):
    rows = q.shape[0]
    size = rows + 2 * ROW_REACH
    low = 2 * ZEROS
    bufs[0, low : low + rows, :] = q
    start, count = ZEROS, size
    for n, gap in enumerate((1, 3, 1, 3)):
        if n == 3:
            start, count = low, rows
        y = (
            bufs[n, start - gap : start - gap + count, :]
            + bufs[n, start : start + count, :]
            + bufs[n, start + gap : start + gap + count, :]
        )
        if n < 3:
            bufs[n + 1, start : start + count, :] = y
    return y


def weigh_kernel(own_ref, la_ref, lb_ref, ra_ref, rb_ref, x_ref, z_ref, ann_ref, *rest, radius, parts):
    outs = rest[:parts]
    lhs, rhs, near, logw, tot, bufs = rest[parts:]
    members, fields, rows, cols = x_ref.shape
    per = cols // GROUP
    planes = members // per
    band = rows // BANDS
    even = lax.rem(lax.axis_index("col"), 2) == 0
    nrow = la_ref.shape[1] // cols
    at = slice(4 * rows, 4 * rows + nrow)
    ia = row_vector(ra_ref[at, :]).astype(jnp.int32)
    ib = row_vector(rb_ref[at, :]).astype(jnp.int32)
    left = jnp.where(even, lb_ref[...], la_ref[...])
    right = jnp.where(even, la_ref[...], lb_ref[...])
    mid = cols // 2
    swapped = [b ^ 1 for b in range(BANDS)]
    near[0] = spread(
        left, jnp.where(even, ib, ia), -cols, 0, mid, range(BANDS), radius, cols, rows, lhs.at[0], rhs.at[0]
    )
    near[1] = spread(
        right, jnp.where(even, ia, ib), cols, mid, mid, swapped, radius, cols, rows, lhs.at[1], rhs.at[1]
    )
    for n in range(bufs.shape[0]):
        for k in range(4):
            bufs[n, k, : 2 * ZEROS, :] = jnp.zeros((2 * ZEROS, cols), f32)
            bufs[n, k, rows + 2 * ZEROS :, :] = jnp.zeros((2 * ZEROS, cols), f32)

    scale = ann_ref[...] * (1.0 / ((ROW_REACH + 1) * (radius + 1)))
    lower = lanes_of((band, cols)) < mid

    def smooth(g, peak):
        for n in range(bufs.shape[0]):
            m = g * bufs.shape[0] + n
            at = pl.ds(pl.multiple_of(m * band, 8), band)
            q = []
            for b in range(0, BANDS, 2):
                l = near[0, at, b * mid : (b + 2) * mid]
                r = near[1, at, b * mid : (b + 2) * mid]
                q.append(own_ref[at, b * cols : (b + 1) * cols] + jnp.where(lower, l, r))
                q.append(
                    own_ref[at, (b + 1) * cols : (b + 2) * cols] + roll_lanes(jnp.where(lower, r, l), mid)
                )
            w = scale * triangle(jnp.concatenate(q, axis=0), bufs.at[n])
            logw[m] = w
            peak = jnp.maximum(peak, w)
        return peak

    peak = lax.fori_loop(0, members // bufs.shape[0], smooth, jnp.full((rows, cols), -jnp.inf, f32))
    tot[fields + 1] = peak
    lane = lanes_of((8, cols))
    grp = lane // GROUP
    border = (lane < EDGE) | (lane >= cols - EDGE)

    def sums(t, carry):
        at = pl.ds(pl.multiple_of(t * 8, 8), 8)
        top = tot[fields + 1, at, :]
        total = jnp.zeros((8, cols), f32)
        s = [jnp.zeros((8, cols), f32)] * fields
        e = [jnp.zeros((8, cols), f32)] * fields
        for q in range(planes):
            packed = None
            for i in range(per):
                m = q * per + i
                w = jnp.exp(logw[m, at, :] - top)
                total = total + w
                for f in range(fields):
                    s[f] = s[f] + w * x_ref[m, f, at, :]
                r = roll_lanes(w, GROUP * i + HALF)
                packed = r if packed is None else jnp.where(grp == i, r, packed)
            for f in range(fields):
                e[f] = e[f] + packed * z_ref[q, f, at, :]
        for f in range(fields):
            for k in (cols // 2, cols // 4, cols // 8):
                e[f] = e[f] + roll_lanes(e[f], k)
            tot[f, at, :] = jnp.where(border, roll_lanes(e[f], cols - HALF), s[f])
        tot[fields, at, :] = total
        return carry

    lax.fori_loop(0, rows // 8, sums, 0, unroll=2)
    part = rows // parts
    me = lax.axis_index("dom")
    for k, ref in enumerate(outs):
        start = pl.multiple_of(partner(me, k, parts) * part, 8)
        ref[...] = tot[:, pl.ds(start, part), :]


def partner(me, k, count):
    return me ^ k if count & (count - 1) == 0 else lax.rem(me + k, count)


def swap(x, k, count):
    return lax.ppermute(x, "dom", [(i, i ^ k if count & (count - 1) == 0 else (i + k) % count) for i in range(count)])


def join_kernel(*refs):
    *ins, out = refs
    fields = out.shape[0]
    peak = functools.reduce(jnp.maximum, [r[fields + 1] for r in ins])
    total = 0.0
    s = [0.0] * fields
    for r in ins:
        e = jnp.exp(r[fields + 1] - peak)
        total = total + r[fields] * e
        for f in range(fields):
            s[f] = s[f] + r[f] * e
    for f in range(fields):
        out[f] = s[f] / total


def place_kernel(*refs):
    *ins, out = refs
    part = ins[0].shape[1]
    me = lax.axis_index("dom")
    count = len(ins)
    for k, r in enumerate(ins):
        source = me if k == 0 else (me ^ k if count & (count - 1) == 0 else lax.rem(me - k + count, count))
        out[:, pl.ds(pl.multiple_of(source * part, 8), part), :] = r[...]


def on_device(ensemble, depth_class, obs_index, obs_value, annealing_exponents):
    members, fields, rows, cols = ensemble.shape
    radius = cols // 2
    per = cols // GROUP
    planes = members // per
    nobs = obs_index.shape[0]
    tall = members * rows // BANDS
    ncol = lax.axis_size("col")
    ndom = lax.axis_size("dom")
    S = jax.ShapeDtypeStruct
    idx = obs_index.reshape(nobs // cols, cols)
    obs = obs_value.reshape(nobs // cols, cols)

    payload = S((4 * rows + 8, cols), f32)
    packed, pa, pb, held = pl.pallas_call(
        pack_kernel,
        out_shape=(S((planes, fields, rows, cols), f32), payload, payload, S((fields, members, rows, cols), f32)),
        in_specs=[HBM] * 3,
        out_specs=(VMEM,) * 4,
        scratch_shapes=[
            pltpu.VMEM(depth_class.shape, jnp.int32),
            pltpu.VMEM(idx.shape, jnp.int32),
            pltpu.SemaphoreType.DMA((fields + 2,)),
        ],
        compiler_params=params(44),
        name="pack",
    )(*[pltpu.with_memory_space_constraint(x, pltpu.HBM) for x in (ensemble, depth_class, idx)])

    inner = [(i, i ^ 1) for i in range(ncol)]
    outer = [(i, (i + 1) % ncol if i % 2 else (i - 1) % ncol) for i in range(ncol)]

    def exchange(a, b):
        rb = lax.ppermute(b, "col", outer)
        ra = lax.ppermute(a, "col", inner)
        return ra, rb

    ra, rb = exchange(pa, pb)
    block = 4
    raw = pl.pallas_call(
        forecast_kernel,
        out_shape=S(ensemble.shape, f32),
        grid=(members // block,),
        in_specs=[
            pl.BlockSpec((fields, block, rows, cols), lambda m: (0, m, 0, 0)),
            pl.BlockSpec((rows, cols), lambda m: (0, 0)),
        ],
        out_specs=pl.BlockSpec((block, fields, rows, cols), lambda m: (m, 0, 0, 0)),
        scratch_shapes=[pltpu.VMEM((8, rows + 2 * ZEROS, cols), f32), pltpu.VMEM((2 * cols, cols), bf16)],
        compiler_params=params(12),
        name="forecast",
    )(held, depth_class)

    edges, loss = pl.pallas_call(
        edge_kernel,
        out_shape=(S((planes, fields, rows, cols), f32), S((members, nobs), f32)),
        in_specs=[VMEM] * 7,
        out_specs=(VMEM, VMEM),
        scratch_shapes=[
            pltpu.VMEM((2, fields + 1, rows, cols), f32),
            pltpu.VMEM((16, rows + 2 * ZEROS, cols), f32),
            pltpu.VMEM((2 * cols, cols), bf16),
            pltpu.VMEM((3, tall, BANDS * cols), bf16),
            pltpu.VMEM((BANDS * cols, nobs), bf16),
            pltpu.VMEM((tall, nobs), f32),
        ],
        compiler_params=params(18),
        name="edges",
    )(ra, rb, packed, depth_class, raw, idx, obs)

    la, lb = exchange(loss, loss)
    own = pl.pallas_call(
        functools.partial(own_kernel, radius=radius, cols=cols, rows=rows),
        out_shape=S((tall, BANDS * cols), f32),
        in_specs=[VMEM, VMEM],
        out_specs=VMEM,
        scratch_shapes=[pltpu.VMEM((3, tall, nobs), bf16), pltpu.VMEM((BANDS * cols, nobs), bf16)],
        compiler_params=params(10),
        name="own",
    )(loss, idx)

    part = S((fields + 2, rows // ndom, cols), f32)
    sums = pl.pallas_call(
        functools.partial(weigh_kernel, radius=radius, parts=ndom),
        out_shape=(part,) * ndom,
        in_specs=[VMEM] * 8,
        out_specs=(VMEM,) * ndom,
        scratch_shapes=[
            pltpu.VMEM((2, 3, tall, nobs), bf16),
            pltpu.VMEM((2, BANDS * cols // 2, nobs), bf16),
            pltpu.VMEM((2, tall, BANDS * cols // 2), f32),
            pltpu.VMEM((members, rows, cols), f32),
            pltpu.VMEM((fields + 2, rows, cols), f32),
            pltpu.VMEM((4, 4, rows + 4 * ZEROS, cols), f32),
        ],
        compiler_params=params(30),
        name="weigh",
    )(own, la, lb, ra, rb, raw, edges, annealing_exponents)

    parts = [sums[0]] + [swap(sums[k], k, ndom) for k in range(1, ndom)]
    mine = pl.pallas_call(
        join_kernel,
        out_shape=S((fields, rows // ndom, cols), f32),
        in_specs=[VMEM] * ndom,
        out_specs=VMEM,
        compiler_params=params(4),
        name="join",
    )(*parts)
    blocks = [mine] + [swap(mine, k, ndom) for k in range(1, ndom)]
    return pl.pallas_call(
        place_kernel,
        out_shape=S((fields, rows, cols), f32),
        in_specs=[VMEM] * ndom,
        out_specs=VMEM,
        compiler_params=params(4),
        name="place",
    )(*blocks)


def solution(mesh):
    in_specs = (P("dom", None, None, "col"), P(None, "col"), P("col"), P("col"), P(None, "col"))
    out_specs = P(None, None, "col")
    return jax.shard_map(
        on_device, mesh=mesh, in_specs=in_specs, out_specs=out_specs, check_vma=False
    )
```

```python
import functools

import jax
import jax.numpy as jnp
from jax import lax
from jax.experimental import pallas as pl
from jax.experimental.pallas import tpu as pltpu
from jax.sharding import PartitionSpec as P

ROW_REACH = 8
TIME_STEP = 0.25
CORIOLIS = 0.2
HALF_STEP = 0.5 * TIME_STEP
GROUP = 16
EDGE = 4
ZEROS = 8
BANDS = 4
HALF = 8
f32 = jnp.float32
bf16 = jnp.bfloat16
VMEM = pl.BlockSpec(memory_space=pltpu.VMEM)
HBM = pl.BlockSpec(memory_space=pltpu.HBM)


def params(mib):
    return pltpu.CompilerParams(vmem_limit_bytes=mib * 1024 * 1024)


def depth_of(cls):
    return 0.5 + 0.25 * cls.astype(f32)


def lanes_of(shape):
    return lax.broadcasted_iota(jnp.int32, shape, len(shape) - 1)


def packed_lanes(shape):
    return (lanes_of(shape) + HALF) & (shape[-1] - 1)


def roll_lanes(x, shift):
    if isinstance(shift, int) and shift % x.shape[-1] == 0:
        return x
    return pltpu.roll(x, shift % x.shape[-1] if isinstance(shift, int) else shift, x.ndim - 1)


def shift_table(cols):
    k = lax.broadcasted_iota(jnp.int32, (2 * cols, cols), 0) & (cols - 1)
    c = lax.broadcasted_iota(jnp.int32, (2 * cols, cols), 1)
    last = cols - 1
    return (jnp.where(k == ((c + 1) & last), HALF_STEP, 0.0) - jnp.where(k == ((c - 1) & last), HALF_STEP, 0.0)).astype(bf16)


def step(fields, depth, pad, slot, table):
    h, u, v, a, b = fields
    rows = h.shape[0]

    def cols(q):
        return roll_lanes(q, -1) - roll_lanes(q, 1)

    def rws(q, n):
        pad[slot + n, ZEROS : ZEROS + rows, :] = q
        return pad[slot + n, ZEROS + 1 : ZEROS + 1 + rows, :] - pad[slot + n, ZEROS - 1 : ZEROS - 1 + rows, :]

    both = jnp.concatenate([a, b], axis=0)
    hi = both.astype(bf16)
    mid = (both - hi.astype(f32)).astype(bf16)
    slopes = jnp.dot(jnp.concatenate([hi, mid], axis=1), table[...], preferred_element_type=f32)
    turn = TIME_STEP * CORIOLIS
    hs = HALF_STEP * h
    un = u - cols(hs) + turn * v
    vn = v - rws(hs, 0) - turn * u
    hn = h - (cols(depth * un) + rws(depth * vn, 1))
    vs = HALF_STEP * vn
    an = a - (un * slopes[:rows] + vs * rws(a, 2))
    bn = b - (un * slopes[rows:] + vs * rws(b, 3))
    return hn, un, vn, an, bn


def prepare(pad, table):
    for n in range(pad.shape[0]):
        pad[n, :ZEROS, :] = jnp.zeros((ZEROS, pad.shape[2]), f32)
        pad[n, pad.shape[1] - ZEROS :, :] = jnp.zeros((ZEROS, pad.shape[2]), f32)
    table[...] = shift_table(table.shape[1])


def two_steps(fields, depth, pad, table, slot=0):
    return step(step(fields, depth, pad, slot, table), depth, pad, slot + 4, table)


def pack_kernel(x_hbm, cls_hbm, idx_hbm, g_ref, pa_ref, pb_ref, buf, cls_ref, idx_ref, sem):
    members, fields, rows, cols = x_hbm.shape
    per = cols // GROUP
    planes = members // per
    even = lax.rem(lax.axis_index("col"), 2) == 0
    copies = [pltpu.make_async_copy(x_hbm.at[:, f], buf.at[f], sem.at[f]) for f in range(fields)]
    copies.append(pltpu.make_async_copy(cls_hbm, cls_ref, sem.at[fields]))
    copies.append(pltpu.make_async_copy(idx_hbm, idx_ref, sem.at[fields + 1]))
    for n in (0, 1, fields, fields + 1):
        copies[n].start()

    def arrive(f):
        copies[f].wait()
        if f + 2 < fields:
            copies[f + 2].start()

    lane = packed_lanes((8, cols))
    grp = lane // GROUP
    sub = (lane % GROUP) // EDGE
    jj = lane % EDGE

    def put(plane, t, right, left):
        at = pl.ds(plane * rows + t * 8, 8)
        pa_ref[at, :] = jnp.where(even, right, left)
        pb_ref[at, :] = jnp.where(even, left, right)

    def edges(f, t):
        at = pl.ds(t * 8, 8)
        right = left = None
        for q in range(planes):
            acc = None
            for i in range(per):
                r = roll_lanes(buf[f, q * per + i, at, :], GROUP * i)
                acc = r if acc is None else jnp.where(grp == i, r, acc)
            g_ref[q, f, at, :] = acc
            r = roll_lanes(acc, EDGE * q - EDGE)
            l = roll_lanes(acc, EDGE * q - HALF)
            right = r if right is None else jnp.where(sub == q, r, right)
            left = l if left is None else jnp.where(sub == q, l, left)
        return right, left

    for f in range(3):
        arrive(f)
        if f == 1:
            copies[fields].wait()

        def body(t, carry, f=f):
            right, left = edges(f, t)
            if f == 1:
                d = depth_of(cls_ref[pl.ds(t * 8, 8), :])
                for n in range(3):
                    e = roll_lanes(d, 3 * n + 3 - HALF)
                    right = jnp.where(lane == EDGE * n, e, right)
                    left = jnp.where(lane == EDGE * n + 3, e, left)
            put(f, t, right, left)
            return carry

        lax.fori_loop(0, rows // 8, body, 0, unroll=4)
    arrive(3)
    arrive(4)

    def tracers(t, carry):
        ra, la = edges(3, t)
        rb, lb = edges(4, t)
        put(3, t, jnp.where(jj >= 2, ra, roll_lanes(rb, -2)), jnp.where(jj < 2, la, roll_lanes(lb, 2)))
        return carry

    lax.fori_loop(0, rows // 8, tracers, 0, unroll=2)
    copies[fields + 1].wait()
    n = idx_ref.shape[0]
    for ref in (pa_ref, pb_ref):
        ref[4 * rows : 4 * rows + 8, :] = jnp.zeros((8, cols), f32)
        ref[4 * rows : 4 * rows + n, :] = idx_ref[...].astype(f32)


def forecast_kernel(x_ref, cls_ref, o_ref, pad, table):
    depth = HALF_STEP * depth_of(cls_ref[...])
    prepare(pad, table)

    def body(m, carry):
        out = two_steps([x_ref[f, m] for f in range(5)], depth, pad, table)
        for f in range(5):
            o_ref[m, f] = out[f]
        return carry

    lax.fori_loop(0, o_ref.shape[0], body, 0, unroll=2)


def pieces_of(x):
    hi = x.astype(bf16)
    rest = x - hi.astype(f32)
    mid = rest.astype(bf16)
    lo = (rest - mid.astype(f32)).astype(bf16)
    return hi, mid, lo


def row_vector(x):
    return jnp.concatenate([x[i : i + 1, :] for i in range(x.shape[0])], axis=1)


def edge_kernel(ra_ref, rb_ref, g_ref, cls_ref, x_ref, idx_ref, obs_ref, z_ref, loss_ref, xs, pad, table, lhs, pick, prod):
    members, _, rows, cols = x_ref.shape
    per = cols // GROUP
    planes = members // per
    even = lax.rem(lax.axis_index("col"), 2) == 0
    lane = lanes_of((rows, cols))
    place = packed_lanes((rows, cols))
    j = place % GROUP
    grp = place // GROUP

    def received(plane):
        at = slice(plane * rows, (plane + 1) * rows)
        a, b = ra_ref[at, :], rb_ref[at, :]
        return jnp.where(even, b, a), jnp.where(even, a, b)

    depth = HALF_STEP * depth_of(cls_ref[...])
    tiled = None
    for i in range(per):
        r = roll_lanes(depth, GROUP * i)
        tiled = r if tiled is None else jnp.where(grp == i, r, tiled)
    ul, ur = received(1)

    def lane_at(x, n):
        at = (n - HALF) % cols
        return x[:, at : at + 1]

    dl = dr = tiled
    for n in range(3):
        dl = jnp.where(j == EDGE + n + 1, HALF_STEP * jnp.broadcast_to(lane_at(ul, EDGE * n), dl.shape), dl)
        dr = jnp.where(j == HALF + n, HALF_STEP * jnp.broadcast_to(lane_at(ur, EDGE * n + 3), dr.shape), dr)
    xs[0, 5] = dl
    xs[1, 5] = dr
    for f in range(5):
        left, right = received(min(f, 3))
        if f == 4:
            left, right = roll_lanes(left, 2), roll_lanes(right, -2)
        xs[0, f] = left
        xs[1, f] = right

    def strips(q, carry):
        left = []
        right = []
        for f in range(5):
            g = g_ref[q, f]
            hl = pltpu.roll(xs[0, f], lax.rem(cols + EDGE - EDGE * q, cols), 1)
            hr = pltpu.roll(xs[1, f], lax.rem(cols + HALF - EDGE * q, cols), 1)
            left.append(jnp.where((j >= EDGE) & (j < HALF), hl, g))
            right.append(jnp.where(j >= HALF, hr, g))
        left = two_steps(left, xs[0, 5], pad, table)
        right = two_steps(right, xs[1, 5], pad, table, 8)
        for f in range(5):
            z_ref[q, f] = jnp.where(j < HALF, right[f], left[f])
        return carry

    prepare(pad, table)
    lax.fori_loop(0, planes, strips, 0)

    idx = row_vector(idx_ref[...])
    obs = row_vector(obs_ref[...])
    nobs = idx.shape[1]
    row, col = lax.shift_right_logical(idx, cols.bit_length() - 1), idx & (cols - 1)
    band = rows // BANDS
    block = sum(jnp.where(row >= band * b, 1, 0) for b in range(1, BANDS))
    here = lax.broadcasted_iota(jnp.int32, (cols, nobs), 0) == col
    for b in range(BANDS):
        pick[b * cols : (b + 1) * cols, :] = jnp.where(here & (block == b), 1.0, 0.0).astype(bf16)
    isrow = lax.broadcasted_iota(jnp.int32, (band, nobs), 0) == row - band * block
    border = (lane < EDGE) | (lane >= cols - EDGE)

    def split(q, carry):
        for i in range(0, per, 2):
            pair = [
                jnp.where(border, roll_lanes(z_ref[q, 0], cols - GROUP * n), x_ref[q * per + n, 0])
                for n in (i, i + 1)
            ]
            at = pl.ds(pl.multiple_of((q * per + i) * band, 16), 2 * band)
            for b in range(BANDS):
                both = jnp.concatenate([h[b * band : (b + 1) * band] for h in pair], axis=0)
                for p, piece in enumerate(pieces_of(both)):
                    lhs[p, at, b * cols : (b + 1) * cols] = piece
        return carry

    lax.fori_loop(0, planes, split, 0)
    prod[...] = sum(jnp.dot(lhs[p], pick[...], preferred_element_type=f32) for p in range(3))

    def gather(q, carry):
        ys = []
        for i in range(per):
            at = pl.ds(pl.multiple_of((q * per + i) * band, 8), band)
            ys.append(jnp.sum(jnp.where(isrow, prod[at, :], 0.0), axis=0, keepdims=True))
        misfit = obs - jnp.concatenate(ys, axis=0)
        loss_ref[pl.ds(pl.multiple_of(q * per, 8), per), :] = -0.5 * misfit * misfit
        return carry

    lax.fori_loop(0, planes, gather, 0)


def spread(loss, idx, offset, first, width, order, radius, cols, rows, lhs, rhs):
    members, n = loss.shape
    band = rows // BANDS
    col = idx & (cols - 1)
    row = lax.shift_right_logical(idx, cols.bit_length() - 1)
    dist = jnp.abs(lax.broadcasted_iota(jnp.int32, (width, n), 0) + (first - offset) - col)
    table = jnp.maximum(0, radius + 1 - dist).astype(f32)
    block = sum(jnp.where(row >= band * b, 1, 0) for b in range(1, BANDS))
    for pos, b in enumerate(order):
        rhs[pos * width : (pos + 1) * width, :] = jnp.where(block == b, table, 0.0).astype(bf16)
    isrow = lax.broadcasted_iota(jnp.int32, (band, n), 0) == row - band * block
    for p, part in enumerate(pieces_of(loss)):
        part = part.astype(f32)
        for m in range(0, members, 2):
            pair = [jnp.where(isrow, part[m + i : m + i + 1, :], 0.0) for i in range(2)]
            lhs[p, band * m : band * (m + 2), :] = jnp.concatenate(pair, axis=0).astype(bf16)
    dims = (((1,), (1,)), ((), ()))
    return sum(lax.dot_general(lhs[p], rhs[...], dims, preferred_element_type=f32) for p in range(3))


def own_kernel(loss_ref, idx_ref, o_ref, lhs, rhs, *, radius, cols, rows):
    o_ref[...] = spread(
        loss_ref[...], row_vector(idx_ref[...]), 0, 0, cols, range(BANDS), radius, cols, rows, lhs, rhs
    )


def triangle(q, bufs):
    rows = q.shape[0]
    size = rows + 2 * ROW_REACH
    low = 2 * ZEROS
    bufs[0, low : low + rows, :] = q
    start, count = ZEROS, size
    for n, gap in enumerate((1, 3, 1, 3)):
        if n == 3:
            start, count = low, rows
        y = (
            bufs[n, start - gap : start - gap + count, :]
            + bufs[n, start : start + count, :]
            + bufs[n, start + gap : start + gap + count, :]
        )
        if n < 3:
            bufs[n + 1, start : start + count, :] = y
    return y


def weigh_kernel(own_ref, la_ref, lb_ref, ra_ref, rb_ref, x_ref, z_ref, ann_ref, *rest, radius, parts):
    outs = rest[:parts]
    lhs, rhs, near, logw, tot, bufs = rest[parts:]
    members, fields, rows, cols = x_ref.shape
    per = cols // GROUP
    planes = members // per
    band = rows // BANDS
    even = lax.rem(lax.axis_index("col"), 2) == 0
    nrow = la_ref.shape[1] // cols
    at = slice(4 * rows, 4 * rows + nrow)
    ia = row_vector(ra_ref[at, :]).astype(jnp.int32)
    ib = row_vector(rb_ref[at, :]).astype(jnp.int32)
    left = jnp.where(even, lb_ref[...], la_ref[...])
    right = jnp.where(even, la_ref[...], lb_ref[...])
    mid = cols // 2
    swapped = [b ^ 1 for b in range(BANDS)]
    near[0] = spread(
        left, jnp.where(even, ib, ia), -cols, 0, mid, range(BANDS), radius, cols, rows, lhs.at[0], rhs.at[0]
    )
    near[1] = spread(
        right, jnp.where(even, ia, ib), cols, mid, mid, swapped, radius, cols, rows, lhs.at[1], rhs.at[1]
    )
    for n in range(bufs.shape[0]):
        for k in range(4):
            bufs[n, k, : 2 * ZEROS, :] = jnp.zeros((2 * ZEROS, cols), f32)
            bufs[n, k, rows + 2 * ZEROS :, :] = jnp.zeros((2 * ZEROS, cols), f32)

    scale = ann_ref[...] * (1.0 / ((ROW_REACH + 1) * (radius + 1)))
    lower = lanes_of((band, cols)) < mid

    def smooth(g, peak):
        for n in range(bufs.shape[0]):
            m = g * bufs.shape[0] + n
            at = pl.ds(pl.multiple_of(m * band, 8), band)
            q = []
            for b in range(0, BANDS, 2):
                l = near[0, at, b * mid : (b + 2) * mid]
                r = near[1, at, b * mid : (b + 2) * mid]
                q.append(own_ref[at, b * cols : (b + 1) * cols] + jnp.where(lower, l, r))
                q.append(
                    own_ref[at, (b + 1) * cols : (b + 2) * cols] + roll_lanes(jnp.where(lower, r, l), mid)
                )
            w = scale * triangle(jnp.concatenate(q, axis=0), bufs.at[n])
            logw[m] = w
            peak = jnp.maximum(peak, w)
        return peak

    peak = lax.fori_loop(0, members // bufs.shape[0], smooth, jnp.full((rows, cols), -jnp.inf, f32))
    tot[fields] = peak
    lane = lanes_of((8, cols))
    grp = packed_lanes((8, cols)) // GROUP
    border = (lane < EDGE) | (lane >= cols - EDGE)

    def sums(t, carry):
        at = pl.ds(pl.multiple_of(t * 8, 8), 8)
        top = tot[fields, at, :]
        total = jnp.zeros((8, cols), f32)
        s = [jnp.zeros((8, cols), f32)] * fields
        e = [jnp.zeros((8, cols), f32)] * fields
        for q in range(planes):
            packed = None
            for i in range(per):
                m = q * per + i
                w = jnp.exp(logw[m, at, :] - top)
                total = total + w
                for f in range(fields):
                    s[f] = s[f] + w * x_ref[m, f, at, :]
                r = roll_lanes(w, GROUP * i)
                packed = r if packed is None else jnp.where(grp == i, r, packed)
            for f in range(fields):
                e[f] = e[f] + packed * z_ref[q, f, at, :]
        inverse = 1.0 / total
        for f in range(fields):
            for k in (cols // 2, cols // 4, cols // 8):
                e[f] = e[f] + roll_lanes(e[f], k)
            tot[f, at, :] = jnp.where(border, e[f], s[f]) * inverse
        tot[fields, at, :] = top + jnp.log(total)
        return carry

    lax.fori_loop(0, rows // 8, sums, 0, unroll=2)
    part = rows // parts
    me = lax.axis_index("dom")
    for k, ref in enumerate(outs):
        start = pl.multiple_of(partner(me, k, parts) * part, 8)
        ref[...] = tot[:, pl.ds(start, part), :]


def partner(me, k, count):
    return me ^ k if count & (count - 1) == 0 else lax.rem(me + k, count)


def swap(x, k, count):
    return lax.ppermute(x, "dom", [(i, i ^ k if count & (count - 1) == 0 else (i + k) % count) for i in range(count)])


def join_kernel(*refs):
    *ins, out = refs
    fields = out.shape[0]
    peak = functools.reduce(jnp.maximum, [r[fields] for r in ins])
    total = 0.0
    s = [0.0] * fields
    for r in ins:
        e = jnp.exp(r[fields] - peak)
        total = total + e
        for f in range(fields):
            s[f] = s[f] + r[f] * e
    for f in range(fields):
        out[f] = s[f] / total


def place_kernel(*refs):
    *ins, out = refs
    part = ins[0].shape[1]
    me = lax.axis_index("dom")
    count = len(ins)
    for k, r in enumerate(ins):
        source = me if k == 0 else (me ^ k if count & (count - 1) == 0 else lax.rem(me - k + count, count))
        out[:, pl.ds(pl.multiple_of(source * part, 8), part), :] = r[...]


def on_device(ensemble, depth_class, obs_index, obs_value, annealing_exponents):
    members, fields, rows, cols = ensemble.shape
    radius = cols // 2
    per = cols // GROUP
    planes = members // per
    nobs = obs_index.shape[0]
    tall = members * rows // BANDS
    ncol = lax.axis_size("col")
    ndom = lax.axis_size("dom")
    S = jax.ShapeDtypeStruct
    idx = obs_index.reshape(nobs // cols, cols)
    obs = obs_value.reshape(nobs // cols, cols)

    payload = S((4 * rows + 8, cols), f32)
    packed, pa, pb, held = pl.pallas_call(
        pack_kernel,
        out_shape=(S((planes, fields, rows, cols), f32), payload, payload, S((fields, members, rows, cols), f32)),
        in_specs=[HBM] * 3,
        out_specs=(VMEM,) * 4,
        scratch_shapes=[
            pltpu.VMEM(depth_class.shape, jnp.int32),
            pltpu.VMEM(idx.shape, jnp.int32),
            pltpu.SemaphoreType.DMA((fields + 2,)),
        ],
        compiler_params=params(44),
        name="pack",
    )(*[pltpu.with_memory_space_constraint(x, pltpu.HBM) for x in (ensemble, depth_class, idx)])

    inner = [(i, i ^ 1) for i in range(ncol)]
    outer = [(i, (i + 1) % ncol if i % 2 else (i - 1) % ncol) for i in range(ncol)]

    def exchange(a, b):
        rb = lax.ppermute(b, "col", outer)
        ra = lax.ppermute(a, "col", inner)
        return ra, rb

    ra, rb = exchange(pa, pb)
    raw = pl.pallas_call(
        forecast_kernel,
        out_shape=S(ensemble.shape, f32),
        in_specs=[VMEM, VMEM],
        out_specs=VMEM,
        scratch_shapes=[pltpu.VMEM((8, rows + 2 * ZEROS, cols), f32), pltpu.VMEM((2 * cols, cols), bf16)],
        compiler_params=params(12),
        name="forecast",
    )(held, depth_class)

    edges, loss = pl.pallas_call(
        edge_kernel,
        out_shape=(S((planes, fields, rows, cols), f32), S((members, nobs), f32)),
        in_specs=[VMEM] * 7,
        out_specs=(VMEM, VMEM),
        scratch_shapes=[
            pltpu.VMEM((2, fields + 1, rows, cols), f32),
            pltpu.VMEM((16, rows + 2 * ZEROS, cols), f32),
            pltpu.VMEM((2 * cols, cols), bf16),
            pltpu.VMEM((3, tall, BANDS * cols), bf16),
            pltpu.VMEM((BANDS * cols, nobs), bf16),
            pltpu.VMEM((tall, nobs), f32),
        ],
        compiler_params=params(18),
        name="edges",
    )(ra, rb, packed, depth_class, raw, idx, obs)

    la, lb = exchange(loss, loss)
    own = pl.pallas_call(
        functools.partial(own_kernel, radius=radius, cols=cols, rows=rows),
        out_shape=S((tall, BANDS * cols), f32),
        in_specs=[VMEM, VMEM],
        out_specs=VMEM,
        scratch_shapes=[pltpu.VMEM((3, tall, nobs), bf16), pltpu.VMEM((BANDS * cols, nobs), bf16)],
        compiler_params=params(10),
        name="own",
    )(loss, idx)

    part = S((fields + 1, rows // ndom, cols), f32)
    sums = pl.pallas_call(
        functools.partial(weigh_kernel, radius=radius, parts=ndom),
        out_shape=(part,) * ndom,
        in_specs=[VMEM] * 8,
        out_specs=(VMEM,) * ndom,
        scratch_shapes=[
            pltpu.VMEM((2, 3, tall, nobs), bf16),
            pltpu.VMEM((2, BANDS * cols // 2, nobs), bf16),
            pltpu.VMEM((2, tall, BANDS * cols // 2), f32),
            pltpu.VMEM((members, rows, cols), f32),
            pltpu.VMEM((fields + 1, rows, cols), f32),
            pltpu.VMEM((4, 4, rows + 4 * ZEROS, cols), f32),
        ],
        compiler_params=params(30),
        name="weigh",
    )(own, la, lb, ra, rb, raw, edges, annealing_exponents)

    parts = [swap(sums[k], k, ndom) if k else sums[0] for k in range(ndom - 1, -1, -1)]
    mine = pl.pallas_call(
        join_kernel,
        out_shape=S((fields, rows // ndom, cols), f32),
        in_specs=[VMEM] * ndom,
        out_specs=VMEM,
        compiler_params=params(4),
        name="join",
    )(*parts)
    blocks = [mine] + [swap(mine, k, ndom) for k in range(1, ndom)]
    return pl.pallas_call(
        place_kernel,
        out_shape=S((fields, rows, cols), f32),
        in_specs=[VMEM] * ndom,
        out_specs=VMEM,
        compiler_params=params(4),
        name="place",
    )(*blocks)


def solution(mesh):
    in_specs = (P("dom", None, None, "col"), P(None, "col"), P("col"), P("col"), P(None, "col"))
    out_specs = P(None, None, "col")
    return jax.shard_map(
        on_device, mesh=mesh, in_specs=in_specs, out_specs=out_specs, check_vma=False
    )
```
